256 devices in a mesh: row: 16 (over x, z_lo), col: 16 (over z_hi, y, core).
Axes of the slice: x: 4, y: 4, z: 8 (z_hi: 2, z_lo: 4; z = z_hi * 4 + z_lo), core: 2. Of those that a mesh axis runs over, the one named last changes fastest.
Arguments:
- factors: bfloat16 [32768, 256], P(('row', 'col')), may hold values from -1.5 to 1.5
- cores: bfloat16 [8, 256, 256], replicated, may hold values from -0.375 to 0.375
- tiles: bfloat16 [8192, 256, 256], P(('row', 'col')), may hold values from -6 to 6
- tile_coords: int32 [8192, 3], P(('row', 'col')), may hold values from 0 to 7, as said below
- tile_counts: int32 [256], P(('row', 'col')), may hold values from 1 to 32, as said below
Outputs:
- gradient: float32 [32768, 256], P(('row', 'col'))
The draws below stay inside these ranges and needn't reach their ends.
Inputs may be any that keep to these rules, and one draw needn't show every extreme that they name: `tile_coords`: column 0 is a relation below 8, column 1 below 8, column 2 below 8; within one device no two slots have the same three coordinates. `tile_counts`: some device has all 32 slots live.
All inputs are finite; a program needn't handle non-finite values.
Results may differ from the reference program's by a relative error of at most 0.0011.
Values may be sent and summed in bfloat16 or wider, within the bound.
A program may use at most 128 MiB of HBM per device.

```python
import jax
import jax.numpy as jnp
from jax import lax

RANK = 256
RELS = 8
TILE = 256
BLK = 8
CAP = 32
BLK_COL = 8
NENT = 32768
N_ROW = 16
N_COL = 16
DEVICES = 256


def draw_tile_coords(key, part):
    positions = RELS * BLK * BLK_COL
    keys = jax.random.split(jax.random.fold_in(key, 11), DEVICES)

    def one_device(dev_key):
        return jax.random.permutation(dev_key, positions)[:CAP]
    picked = jax.vmap(one_device)(keys).astype(jnp.int32)
    relation = picked // (BLK * BLK_COL)
    src_index = picked // BLK_COL % BLK
    tgt_index = picked % BLK_COL
    return jnp.stack([relation, src_index, tgt_index], axis=-1).reshape(DEVICES * CAP, 3).astype(jnp.int32)


def draw_tile_counts(key, part):
    key_first = jax.random.fold_in(key, 21)
    key_second = jax.random.fold_in(key, 22)
    key_full = jax.random.fold_in(key, 23)
    first = jax.random.randint(key_first, (DEVICES,), 0, CAP)
    second = jax.random.randint(key_second, (DEVICES,), 0, CAP)
    counts = 1 + jnp.minimum(first, second)
    busiest = jax.random.randint(key_full, (), 0, DEVICES)
    return counts.at[busiest].set(CAP).astype(jnp.int32)


def level_of(rng, extent, shards, smallest, largest):
    def one(dim, shards_of):
        steps = jax.random.uniform(jax.random.fold_in(jax.random.fold_in(rng, 6), dim), (shards_of,), jnp.float32, smallest / len(shards), largest / len(shards))
        return jnp.repeat(jnp.exp(steps), extent[dim] // shards_of).reshape((-1,) + (1,) * (len(extent) - dim - 1))

    level = one(*shards[0])
    for cut in shards[1:]:
        level = level * one(*cut)
    return level


def gaussian(stream_key, extent, scale, bound, cuts=(), kind=jnp.bfloat16):
    factor_of = level_of(stream_key, extent, cuts, -0.22, 0.18) if cuts else 1.0
    drawn = jax.random.normal(stream_key, extent, jnp.float32) * scale * factor_of
    return jnp.minimum(jnp.maximum(drawn, -bound), bound).astype(kind)


def setup_inputs(seed: int = 0) -> dict:
    streams_of = jax.random.split(jax.random.key(seed), 6)
    return {
        "factors": gaussian(streams_of[0], (NENT, RANK), 0.25, 1.5, ((0, 256),)),
        "cores": gaussian(streams_of[1], (RELS, RANK, RANK), RANK ** -0.5, 0.375),
        "tiles": gaussian(streams_of[2], (DEVICES * CAP, TILE, TILE), 1.0, 6.0, ((0, 256),)),
        "tile_coords": draw_tile_coords(jax.random.fold_in(streams_of[5], 71), 0),
        "tile_counts": draw_tile_counts(jax.random.fold_in(streams_of[5], 71), 0),
    }


weight_decay = 1.0


def reference(factors, cores, tiles, tile_coords, tile_counts):
    fac32 = factors.astype(jnp.float32)
    core32 = cores.astype(jnp.float32)
    blocks_all = NENT // TILE
    left_core = jnp.einsum('nr,krs->kns', fac32, core32).astype(jnp.bfloat16).reshape(RELS, blocks_all, TILE, RANK)
    right_core = jnp.einsum('nr,ksr->kns', fac32, core32).astype(jnp.bfloat16).reshape(RELS, blocks_all, TILE, RANK)
    fac_blocks = factors.reshape(blocks_all, TILE, RANK)

    def device_pass(device, grads):
        row_pos = device // N_COL
        col_pos = device % N_COL
        live_count = tile_counts[device]

        def group_pass(group, grads):
            start = (device * CAP + group * 8).astype(jnp.int32)
            coords = lax.dynamic_slice_in_dim(tile_coords, start, 8, 0)
            values = lax.dynamic_slice_in_dim(tiles, start, 8, 0).astype(jnp.float32)
            is_live = (group * 8 + jnp.arange(8, dtype=jnp.int32)) < live_count
            relation = coords[:, 0]
            src_block = row_pos * BLK + coords[:, 1]
            tgt_block = col_pos * BLK_COL + coords[:, 2]
            left = left_core[relation, src_block].astype(jnp.float32)
            right = fac_blocks[tgt_block].astype(jnp.float32)
            right_rel = right_core[relation, tgt_block].astype(jnp.float32)
            predicted = jnp.einsum('gtr,gur->gtu', left, right)
            resid_half = jnp.where(is_live[:, None, None], values - predicted, 0.0).astype(jnp.bfloat16)
            resid = lax.optimization_barrier(resid_half).astype(jnp.float32)
            src_grad = jnp.einsum('gtu,gur->gtr', resid, right_rel)
            tgt_grad = jnp.einsum('gtu,gtr->gur', resid, left)
            return grads.at[src_block].add(src_grad).at[tgt_block].add(tgt_grad)

        return lax.fori_loop(0, (live_count + 7) // 8, group_pass, grads)

    grads = jnp.zeros((blocks_all, TILE, RANK), jnp.float32)
    grads = lax.fori_loop(0, N_ROW * N_COL, device_pass, grads)
    return weight_decay * fac32 - grads.reshape(NENT, RANK) / TILE
```

```python
import jax
import jax.numpy as jnp
from jax import lax
from jax.experimental import pallas as pl
from jax.experimental.pallas import tpu as pltpu
from jax.sharding import PartitionSpec as P

weight_decay = 1.0
MESH = pl.DeviceIdType.MESH
ROWS = 128
HALF = 64
TILE = 256
CAP = 32
F32 = jnp.float32
BF16 = jnp.bfloat16


class Place:
    def __init__(self):
        row, col = lax.axis_index("row"), lax.axis_index("col")
        self.row, self.col = row, col
        self.x, self.zl = row // 4, row % 4
        self.zh, self.y, self.c = col // 8, (col // 2) % 4, col % 2

    def at_row(self, x, zl):
        return ((x % 4) * 4 + zl % 4, self.col)

    def at_col(self, zh, y, c):
        return (self.row, zh * 8 + (y % 4) * 2 + c)

    def meet(self):
        x, zl, zh, y, c = self.x, self.zl, self.zh, self.y, self.c
        self.xp, self.xm = self.at_row(x + 1, zl), self.at_row(x + 3, zl)
        self.zls = [self.at_row(x, zl + d) for d in (1, 2, 3)]
        self.yp, self.ym = self.at_col(zh, y + 1, c), self.at_col(zh, y + 3, c)
        self.far = self.at_col(1 - zh, y, c)
        self.core = self.at_col(zh, y, 1 - c)
        self.flip = (self.col, self.row)
        barrier = pltpu.get_barrier_semaphore()
        peers = [self.xp, self.xm, *self.zls, self.yp, self.ym, self.far, self.core]
        for peer in peers:
            pl.semaphore_signal(barrier, inc=1, device_id=peer, device_id_type=MESH)

        @pl.when(self.row != self.col)
        def _():
            pl.semaphore_signal(barrier, inc=1, device_id=self.flip, device_id_type=MESH)

        pl.semaphore_wait(barrier, len(peers) + jnp.where(self.row != self.col, 1, 0))


class Wires:
    def __init__(self, ssem, rsem):
        self.ssem, self.rsem, self.sent = ssem, rsem, []

    def make(self, n, src, dst, device):
        return pltpu.make_async_remote_copy(
            src_ref=src,
            dst_ref=dst,
            send_sem=self.ssem.at[n],
            recv_sem=self.rsem.at[n],
            device_id=device,
            device_id_type=MESH,
        )

    def send(self, n, src, dst, device):
        copy = self.make(n, src, dst, device)
        copy.start()
        self.sent.append(copy)

    def landed(self, n, dst, device):
        self.make(n, dst, dst, device).wait_recv()

    def drain(self):
        for copy in self.sent:
            copy.wait_send()


def slot(ref, index, first=0, size=ROWS):
    return ref.at[pl.ds(pl.multiple_of(index * ROWS + first, HALF), size), :]


def gather_kernel(fac, src, tgt, ssem, rsem):
    p = Place()
    p.meet()
    w = Wires(ssem, rsem)
    x, zl, zh, y, c, row, col = p.x, p.zl, p.zh, p.y, p.c, p.row, p.col
    T, FAR, CORE, ZL, YD, YR, XD, XR = 0, 1, 2, 10, 13, 17, 21, 29
    off_diag = row != col
    turn = w.make(T, fac, slot(tgt, row * 0 + col), p.flip)

    @pl.when(off_diag)
    def _():
        turn.start()

    w.send(FAR, fac, slot(src, col), p.far)
    w.send(YD + 0, fac, slot(src, col), p.yp)
    w.send(YD + 1, fac, slot(src, col), p.ym)
    w.send(CORE + 0, fac, slot(src, col), p.core)
    src[pl.ds(pl.multiple_of(col * ROWS, ROWS), ROWS), :] = fac[...]

    @pl.when(row == col)
    def _():
        tgt[pl.ds(pl.multiple_of(row * ROWS, ROWS), ROWS), :] = fac[...]

    @pl.when(off_diag)
    def _():
        w.landed(T, slot(tgt, row), p.flip)

    mine = slot(tgt, row)
    w.send(XD + 0, mine, mine, p.xp)
    w.send(XD + 1, mine, mine, p.xm)
    for d in (1, 2, 3):
        w.send(ZL + d - 1, mine, mine, p.zls[d - 1])

    def at(yy, hh):
        return hh * 8 + (yy % 4) * 2 + c

    def y_pass(h, hh, core_base):
        left, right, far = at(y + 3, hh), at(y + 1, hh), at(y + 2, hh)
        w.landed(YD + 2 * h, slot(src, left), p.ym)
        w.send(YR + 2 * h, slot(src, left, 0, HALF), slot(src, left, 0, HALF), p.yp)
        w.send(core_base, slot(src, left), slot(src, left), p.core)
        w.landed(YD + 2 * h + 1, slot(src, right), p.yp)
        w.send(YR + 2 * h + 1, slot(src, right, HALF, HALF), slot(src, right, HALF, HALF), p.ym)
        w.send(core_base + 1, slot(src, right), slot(src, right), p.core)

    def y_last(h, hh, core_base):
        far = at(y + 2, hh)
        w.landed(YR + 2 * h, slot(src, far, 0, HALF), p.ym)
        w.landed(YR + 2 * h + 1, slot(src, far, HALF, HALF), p.yp)
        w.send(core_base + 2, slot(src, far), slot(src, far), p.core)

    w.landed(FAR, slot(src, at(y, 1 - zh)), p.far)
    other = slot(src, at(y, 1 - zh))
    w.send(YD + 2, other, other, p.yp)
    w.send(YD + 3, other, other, p.ym)
    w.send(CORE + 1, other, other, p.core)
    y_pass(0, zh, CORE + 2)
    for d in (1, 2, 3):
        got = slot(tgt, x * 4 + (zl + 4 - d) % 4)
        w.landed(ZL + d - 1, got, p.zls[3 - d])
        w.send(XD + 2 * d, got, got, p.xp)
        w.send(XD + 2 * d + 1, got, got, p.xm)
    for d in (0, 1, 2, 3):
        k = (zl + 4 - d) % 4
        left, right = ((x + 3) % 4) * 4 + k, ((x + 1) % 4) * 4 + k
        w.landed(XD + 2 * d, slot(tgt, left), p.xm)
        w.send(XR + 2 * d, slot(tgt, left, 0, HALF), slot(tgt, left, 0, HALF), p.xp)
        w.landed(XD + 2 * d + 1, slot(tgt, right), p.xp)
        w.send(XR + 2 * d + 1, slot(tgt, right, HALF, HALF), slot(tgt, right, HALF, HALF), p.xm)
        if d == 0:
            y_pass(1, 1 - zh, CORE + 5)
            y_last(0, zh, CORE + 2)
            y_last(1, 1 - zh, CORE + 5)
    for d in (0, 1, 2, 3):
        far = ((x + 2) % 4) * 4 + (zl + 4 - d) % 4
        w.landed(XR + 2 * d, slot(tgt, far, 0, HALF), p.xm)
        w.landed(XR + 2 * d + 1, slot(tgt, far, HALF, HALF), p.xp)

    def partner(yy, hh):
        return slot(src, hh * 8 + (yy % 4) * 2 + 1 - c)

    arrivals = [(y, zh), (y, 1 - zh)]
    arrivals += [(y + d, hh) for hh in (zh, 1 - zh) for d in (3, 1, 2)]
    for n, (yy, hh) in enumerate(arrivals):
        w.landed(CORE + n, partner(yy, hh), p.core)

    @pl.when(off_diag)
    def _():
        turn.wait_send()

    w.drain()


def tile_kernel(coords, count, src, tgt, cores, tiles, gsrc, gtgt, held, sem):
    live = count[0]
    for s in range(CAP):
        @pl.when(s < live)
        def _():
            pltpu.make_async_copy(tiles.at[s], held.at[s], sem.at[s]).start()

    gsrc[...] = jnp.zeros_like(gsrc)
    gtgt[...] = jnp.zeros_like(gtgt)

    def rows(i):
        return pl.ds(pl.multiple_of(i * TILE, TILE), TILE)

    def dot(a, b, ca, cb):
        return lax.dot_general(a, b, (((ca,), (cb,)), ((), ())), preferred_element_type=F32)

    def step(i, _):
        s = [2 * i, 2 * i + 1]
        for u in s:
            @pl.when(u < live)
            def _():
                pltpu.make_async_copy(tiles.at[u], held.at[u], sem.at[u]).wait()
        rel = [cores[coords[u * 3 + 0]] for u in s]
        a = [rows(coords[u * 3 + 1]) for u in s]
        b = [rows(coords[u * 3 + 2]) for u in s]
        left = [dot(src[a[n], :], rel[n], 1, 0).astype(BF16) for n in (0, 1)]
        right = [dot(tgt[b[n], :], rel[n], 1, 1).astype(BF16) for n in (0, 1)]
        resid = []
        for n in (0, 1):
            predicted = dot(left[n], tgt[b[n], :], 1, 1)
            diff = held[s[n]].astype(F32) - predicted
            resid.append(jnp.where(s[n] < live, diff, 0.0).astype(BF16))
        for n in (0, 1):
            gsrc[a[n], :] += dot(resid[n], right[n], 1, 0)
            gtgt[b[n], :] += dot(resid[n], left[n], 0, 0)
        return 0

    lax.fori_loop(0, (live + 1) // 2, step, 0)


def reduce_kernel(fac, src, tgt, out, xrelay, xdone, zin, core_in, yrelay, ydone, send_z, far_in, send_f, send_t, turn_in, ssem, rsem):
    p = Place()
    p.meet()
    w = Wires(ssem, rsem)
    x, zl, zh, y, c, row, col = p.x, p.zl, p.zh, p.y, p.c, p.row, p.col
    off_diag = row != col
    XS, XA, XD, ZL, CORE, YS, YA, YD, FAR, T = 0, 8, 16, 24, 27, 35, 39, 43, 47, 48
    A, B = 0, HALF

    def part(ref, index, first=0, size=ROWS):
        return ref[pl.ds(pl.multiple_of(index * ROWS + first, HALF), size), :]

    def xs(q, d):
        return ((x + q) % 4) * 4 + (zl + d) % 4

    order = (1, 2, 3, 0)
    for d in order:
        w.send(XS + 2 * d, slot(tgt, xs(2, d), A, HALF), xrelay.at[2 * d], p.xp)
        w.send(XS + 2 * d + 1, slot(tgt, xs(2, d), B, HALF), xrelay.at[2 * d + 1], p.xm)
    for d in order:
        w.send(XD + 2 * d, slot(tgt, xs(1, d), B, HALF), xdone.at[4 * d + 0], p.xp)
        w.send(XD + 2 * d + 1, slot(tgt, xs(3, d), A, HALF), xdone.at[4 * d + 1], p.xm)

    def ys(q, h, cc):
        return ((zh + h) % 2) * 8 + ((y + q) % 4) * 2 + cc

    quarters = (2, 1, 3, 0)
    for n, q in enumerate(quarters):
        for h in (1, 0):
            m = 2 * n + h
            w.send(CORE + m, slot(src, ys(q, h, 1 - c)), core_in.at[m], p.core)
    for n, q in enumerate(quarters):
        for h in (1, 0):
            m = 2 * n + h
            w.landed(CORE + m, core_in.at[m], p.core)
            core_in[m] += part(src, ys(q, h, c))
            if q == 2:
                w.send(YS + 2 * h, core_in.at[m, pl.ds(A, HALF), :], yrelay.at[2 * h], p.yp)
                w.send(YS + 2 * h + 1, core_in.at[m, pl.ds(B, HALF), :], yrelay.at[2 * h + 1], p.ym)
            if q == 1:
                w.send(YD + 2 * h, core_in.at[m, pl.ds(B, HALF), :], ydone.at[4 * h + 0], p.yp)
            if q == 3:
                w.send(YD + 2 * h + 1, core_in.at[m, pl.ds(A, HALF), :], ydone.at[4 * h + 1], p.ym)
    for d in order:
        w.landed(XS + 2 * d, xrelay.at[2 * d], p.xm)
        xrelay[2 * d] += part(tgt, xs(1, d), A, HALF)
        w.send(XA + 2 * d, xrelay.at[2 * d], xdone.at[4 * d + 2], p.xp)
        w.landed(XS + 2 * d + 1, xrelay.at[2 * d + 1], p.xp)
        xrelay[2 * d + 1] += part(tgt, xs(3, d), B, HALF)
        w.send(XA + 2 * d + 1, xrelay.at[2 * d + 1], xdone.at[4 * d + 3], p.xm)
    for h in (1, 0):
        w.landed(YS + 2 * h, yrelay.at[2 * h], p.ym)
        yrelay[2 * h] += core_in[2 + h, pl.ds(A, HALF), :]
        w.send(YA + 2 * h, yrelay.at[2 * h], ydone.at[4 * h + 2], p.yp)
        w.landed(YS + 2 * h + 1, yrelay.at[2 * h + 1], p.yp)
        yrelay[2 * h + 1] += core_in[4 + h, pl.ds(B, HALF), :]
        w.send(YA + 2 * h + 1, yrelay.at[2 * h + 1], ydone.at[4 * h + 3], p.ym)

    def y_sum(h):
        w.landed(YD + 2 * h, ydone.at[4 * h + 0], p.ym)
        w.landed(YD + 2 * h + 1, ydone.at[4 * h + 1], p.yp)
        w.landed(YA + 2 * h, ydone.at[4 * h + 2], p.ym)
        w.landed(YA + 2 * h + 1, ydone.at[4 * h + 3], p.yp)
        own = core_in[6 + h]
        top = own[:HALF] + ydone[4 * h + 1] + ydone[4 * h + 2]
        low = own[HALF:] + ydone[4 * h + 0] + ydone[4 * h + 3]
        return jnp.concatenate([top, low], axis=0)

    def x_sum(d):
        w.landed(XD + 2 * d, xdone.at[4 * d + 0], p.xm)
        w.landed(XD + 2 * d + 1, xdone.at[4 * d + 1], p.xp)
        w.landed(XA + 2 * d, xdone.at[4 * d + 2], p.xm)
        w.landed(XA + 2 * d + 1, xdone.at[4 * d + 3], p.xp)
        own = part(tgt, xs(0, d))
        top = own[:HALF] + xdone[4 * d + 1] + xdone[4 * d + 2]
        low = own[HALF:] + xdone[4 * d + 0] + xdone[4 * d + 3]
        return jnp.concatenate([top, low], axis=0)

    send_f[...] = y_sum(1)
    w.send(FAR, send_f, far_in, p.far)
    for d in (1, 2, 3):
        send_z[d - 1] = x_sum(d)
        w.send(ZL + d - 1, send_z.at[d - 1], zin.at[d - 1], p.zls[d - 1])
    total = x_sum(0)
    for d in (1, 2, 3):
        w.landed(ZL + d - 1, zin.at[d - 1], p.zls[3 - d])
        total = total + zin[d - 1]
    send_t[...] = total
    turn = w.make(T, send_t, turn_in, p.flip)

    @pl.when(off_diag)
    def _():
        turn.start()

    @pl.when(row == col)
    def _():
        turn_in[...] = send_t[...]

    near = y_sum(0)
    w.landed(FAR, far_in, p.far)
    near = near + far_in[...]

    @pl.when(off_diag)
    def _():
        turn.wait()

    summed = near + turn_in[...]
    out[...] = weight_decay * fac[...].astype(F32) - summed * (1.0 / TILE)
    w.drain()


def local(factors, cores, tiles, tile_coords, tile_counts):
    vmem = pl.BlockSpec(memory_space=pltpu.VMEM)
    smem = pl.BlockSpec(memory_space=pltpu.SMEM)
    hbm = pl.BlockSpec(memory_space=pl.ANY)
    dma = pltpu.SemaphoreType.DMA
    rank = factors.shape[1]
    block = 16 * ROWS
    src, tgt = pl.pallas_call(
        gather_kernel,
        out_shape=(jax.ShapeDtypeStruct((block, rank), BF16),) * 2,
        in_specs=[vmem],
        out_specs=(vmem, vmem),
        scratch_shapes=[dma((37,)), dma((37,))],
        compiler_params=pltpu.CompilerParams(collective_id=0, has_side_effects=True),
        name="gather",
    )(factors)
    gsrc, gtgt = pl.pallas_call(
        tile_kernel,
        out_shape=(jax.ShapeDtypeStruct((block, rank), F32),) * 2,
        in_specs=[smem, smem, vmem, vmem, vmem, hbm],
        out_specs=(vmem, vmem),
        scratch_shapes=[pltpu.VMEM((CAP, TILE, TILE), BF16), dma((CAP,))],
        name="tiles",
    )(tile_coords.reshape(-1), tile_counts, src, tgt, cores, tiles)
    full, half = (ROWS, rank), (HALF, rank)
    return pl.pallas_call(
        reduce_kernel,
        out_shape=jax.ShapeDtypeStruct(full, F32),
        in_specs=[vmem, vmem, vmem],
        out_specs=vmem,
        scratch_shapes=[
            pltpu.VMEM((8, *half), F32),
            pltpu.VMEM((16, *half), F32),
            pltpu.VMEM((3, *full), F32),
            pltpu.VMEM((8, *full), F32),
            pltpu.VMEM((4, *half), F32),
            pltpu.VMEM((8, *half), F32),
            pltpu.VMEM((3, *full), F32),
            pltpu.VMEM(full, F32),
            pltpu.VMEM(full, F32),
            pltpu.VMEM(full, F32),
            pltpu.VMEM(full, F32),
            dma((49,)),
            dma((49,)),
        ],
        compiler_params=pltpu.CompilerParams(collective_id=1, has_side_effects=True),
        name="reduce",
    )(factors, gsrc, gtgt)


def solution(mesh):
    in_specs = (
        P(("row", "col"), None),
        P(),
        P(("row", "col"), None, None),
        P(("row", "col"), None),
        P(("row", "col")),
    )
    out_specs = P(("row", "col"), None)
    return jax.shard_map(local, mesh=mesh, in_specs=in_specs, out_specs=out_specs, check_vma=False)
```
